256 devices in a mesh: seq: 32 (over z, x_lo, core), mp: 8 (over y, x_hi).
Axes of the slice: x: 4 (x_hi: 2, x_lo: 2; x = x_hi * 2 + x_lo), y: 4, z: 8, core: 2. Of those that a mesh axis runs over, the one named last changes fastest.
Arguments:
- streams: float32 [4096, 3, 4096], P('seq', None, 'mp'), may hold values from -6 to 6
- se_filter: float32 [7, 3, 256], P(None, None, 'mp'), may hold values from -3 to 3
- mr_filter: float32 [128, 256], P(None, 'mp'), may hold values from -1.5 to 1.5
- mr_decay: float32 [256], P('mp'), may hold values from 0.004 to 0.1
- query: float32 [4096, 4096], P('seq', 'mp'), may hold values from -8 to 8
- key: float32 [4096, 4096], P('seq', 'mp'), may hold values from -8 to 8
- value: float32 [4096, 4096], P('seq', 'mp'), may hold values from -6 to 6
- placement_list: int32 [32], replicated, may hold values from 0 to 31, each once
- doc_ids: int32 [4096], replicated, may hold values from 0 to 7, never falling along the last dimension, each value on 1 to 1024 neighbouring positions
- norm_gain: float32 [4096], P('mp'), may hold values from 0.25 to 1.75
Outputs:
- mixed: float32 [4096, 4096], P('seq', 'mp')
The draws below stay inside these ranges and needn't reach their ends.
Inputs may be any that keep to these rules, and one draw needn't show every extreme that they name: placement_list names every stretch once. doc_ids never falls along the sequence; each document holds at most 1024 positions and one holds exactly that many.
All inputs are finite; a program needn't handle non-finite values.
Results may differ from the reference program's by a relative error of at most 0.0003.
Values sent between devices are 32-bit elements; how exact they have to be, the bound alone decides.
No kernel may reach another device: no remote copies, remote signals or barrier semaphores. Data moves between devices by JAX's collectives and lax.ppermute only.
A program may use at most 128 MiB of HBM per device.

```python
import math
import jax
import jax.numpy as jnp
import numpy as np
from jax import lax

CH = 4096
GROUP = 16
GROUPS = 256
SE_LEN = 7
MR_LEN = 128
HEADS = 32
HD = 128
TOK_DEV = 128
TOKENS = 4096
DOCS = 8
N_SEQ = 32


def drawn_pair(key):
    shape = (TOKENS, HEADS * HD)
    keys = jnp.clip(jax.random.normal(jax.random.fold_in(key, 11), shape, jnp.float32), -6.0, 6.0)
    queries = jnp.clip(jax.random.normal(jax.random.fold_in(key, 12), shape, jnp.float32), -6.0, 6.0)
    return (queries, keys)


def draw_query(key, part):
    return drawn_pair(key)[0]


def draw_key(key, part):
    return drawn_pair(key)[1]


def shard_levels(key, dims, cuts, smallest, top_value):
    def one(position, parts):
        steps = jax.random.uniform(jax.random.fold_in(jax.random.fold_in(key, 6), position), (parts,), jnp.float32, smallest / len(cuts), top_value / len(cuts))
        return jnp.repeat(jnp.exp(steps), dims[position] // parts).reshape((-1,) + (1,) * (len(dims) - position - 1))

    loudness = one(*cuts[0])
    for cut in cuts[1:]:
        loudness = loudness * one(*cut)
    return loudness


def profile(amount, total, bound, slope):
    loads = [(1 << 20) // math.isqrt(grade ** slope) + 1 for grade in range(2, amount + 1)]
    surplus, given = total - bound - (amount - 1), [1] * (amount - 1)
    while surplus > 0:
        free = [i for i in range(amount - 1) if given[i] < bound]
        pool, remaining = sum([loads[i] for i in free]), surplus
        for i in free:
            addition = min(bound - given[i], max(1, remaining * loads[i] // pool), surplus)
            given[i] = given[i] + addition
            surplus = surplus - addition
    return np.array([bound] + given)


def uneven(key, number_of, total, limit, lean):
    if number_of == 2:
        one = jax.random.randint(key, (), max(1, total - limit), min(limit, total - 1) + 1)
        return jnp.stack([one, total - one])
    sizes = jnp.asarray(profile(number_of, total, limit, lean), jnp.int32)
    pairs = (number_of - 1) // 2
    giver, receiver = sizes[1:1 + 2 * pairs:2], sizes[2:2 + 2 * pairs:2]
    slack = jnp.minimum(giver - 1, limit - receiver)
    moved = jax.random.randint(jax.random.fold_in(key, 1), (pairs,), 0, 1 << 20) % (slack + 1)
    sizes = sizes.at[1:1 + 2 * pairs:2].set(giver - moved).at[2:2 + 2 * pairs:2].set(receiver + moved)
    return sizes[jax.random.permutation(jax.random.fold_in(key, 2), number_of)]


def normal_values(stream_key, dims, deviation, bound, shards=(), kind=jnp.bfloat16):
    drawn = deviation * jax.random.normal(stream_key, dims, jnp.float32)
    if shards:
        drawn = drawn * shard_levels(stream_key, dims, shards, -0.22, 0.18)
    return jnp.clip(drawn, -bound, bound).astype(kind)


def setup_inputs(seed: int = 0) -> dict:
    splits = jax.random.split(jax.random.key(seed), 11)
    return {
        "streams": normal_values(splits[0], (TOKENS, 3, CH), 1.0, 6.0, ((0, 32), (2, 8)), jnp.float32),
        "se_filter": normal_values(splits[1], (SE_LEN, 3, GROUPS), 0.45, 3.0, ((2, 8),), jnp.float32),
        "mr_filter": normal_values(splits[2], (MR_LEN, GROUPS), 0.25, 1.5, ((1, 8),), jnp.float32),
        "mr_decay": jnp.clip(jnp.exp(math.log(0.1) - 3.218876 * jax.random.uniform(splits[3], (GROUPS,), jnp.float32) ** shard_levels(splits[3], (GROUPS,), ((0, 8),), -0.2, 0.2)), 0.004, 0.1),
        "query": draw_query(jax.random.fold_in(splits[10], 71), 0),
        "key": draw_key(jax.random.fold_in(splits[10], 71), 0),
        "value": normal_values(splits[6], (TOKENS, CH), 1.0, 6.0, ((0, 32), (1, 8)), jnp.float32),
        "placement_list": jax.random.permutation(splits[7], N_SEQ).astype(jnp.int32),
        "doc_ids": jnp.searchsorted(jnp.cumsum(uneven(splits[8], DOCS, TOKENS, TOKENS // 4, 2)), jnp.arange(TOKENS), side="right").astype(jnp.int32),
        "norm_gain": jnp.clip(1.0 + 0.15 * jax.random.normal(splits[9], (CH,), jnp.float32), 0.25, 1.75),
    }


def shifted(x, lag, fill):
    if lag == 0:
        return x
    front = jnp.full((lag,) + x.shape[1:], fill, x.dtype)
    return jnp.concatenate([front, x[:x.shape[0] - lag]], axis=0)

def reference(streams, se_filter, mr_filter, mr_decay, query, key, value, placement_list, doc_ids, norm_gain):
    inverse = jnp.zeros((N_SEQ,), jnp.int32).at[placement_list].set(jnp.arange(N_SEQ, dtype=jnp.int32))

    def natural(x):
        return x.reshape((N_SEQ, TOK_DEV) + x.shape[1:])[inverse].reshape(x.shape)

    def stored(x):
        return x.reshape((N_SEQ, TOK_DEV) + x.shape[1:])[placement_list].reshape(x.shape)
    seq_streams = natural(streams)
    seq_query = natural(query)
    seq_key = natural(key)
    seq_value = natural(value)
    docs = doc_ids.astype(jnp.int32)
    short_taps = jnp.repeat(se_filter, GROUP, axis=2)
    featured = jnp.zeros((TOKENS, 3, CH), jnp.float32)
    for lag in range(SE_LEN):
        same = (shifted(docs, lag, -1) == docs)[:, None, None]
        featured = featured + jnp.where(same, short_taps[lag][None] * shifted(seq_streams, lag, 0.0), 0.0)
    gated = featured[:, 1] * featured[:, 2]
    lags = jnp.arange(MR_LEN, dtype=jnp.float32)[:, None]
    taps = mr_filter * jnp.exp(-mr_decay[None, :] * lags)
    long_taps = jnp.repeat(taps, GROUP, axis=1)
    conv = jnp.zeros((TOKENS, CH), jnp.float32)
    for lag in range(MR_LEN):
        same = (shifted(docs, lag, -1) == docs)[:, None]
        conv = conv + jnp.where(same, long_taps[lag][None] * shifted(gated, lag, 0.0), 0.0)
    hyena = featured[:, 0] * conv
    positions = jnp.arange(TOKENS, dtype=jnp.int32)
    allowed = (positions[None, :] <= positions[:, None]) & (docs[None, :] == docs[:, None])
    heads_q = seq_query.reshape(TOKENS, HEADS, HD).transpose(1, 0, 2)
    heads_k = seq_key.reshape(TOKENS, HEADS, HD).transpose(1, 0, 2)
    heads_v = seq_value.reshape(TOKENS, HEADS, HD).transpose(1, 0, 2)

    def one_head(args):
        qq, kk, vv = args
        scores = jnp.dot(qq, kk.T, precision=lax.Precision.HIGHEST) / jnp.sqrt(jnp.float32(HD))
        scores = jnp.where(allowed, scores, jnp.float32(-1e+30))
        top = lax.optimization_barrier(jnp.max(scores, axis=1, keepdims=True))
        weights = jnp.where(allowed, jnp.exp(scores - top), 0.0)
        total = lax.optimization_barrier(jnp.sum(weights, axis=1, keepdims=True))
        return jnp.dot(weights, vv, precision=lax.Precision.HIGHEST) / total
    attended = lax.map(one_head, (heads_q, heads_k, heads_v)).transpose(1, 0, 2).reshape(TOKENS, CH)
    summed = hyena + attended
    scale = lax.rsqrt(lax.optimization_barrier(jnp.mean(summed * summed, axis=1, keepdims=True)) + 1e-05)
    return stored(summed * scale * norm_gain[None, :])
```

```python
import jax
import jax.numpy as jnp
from jax import lax
from jax.experimental import pallas as pl
from jax.experimental.pallas import tpu as pltpu
from jax.sharding import PartitionSpec as P


N = 32
T = 128
HD = 128
W = 512
NB = 9
SE = 7
FAR = 27
VMEM = pl.BlockSpec(memory_space=pltpu.VMEM)
SMEM = pl.BlockSpec(memory_space=pltpu.SMEM)
ANY = pl.BlockSpec(memory_space=pl.ANY)
HIGHEST = lax.Precision.HIGHEST
F32 = jnp.float32


def iota(shape, dim):
    return lax.broadcasted_iota(jnp.int32, shape, dim)


def column(row):
    eye = iota((T, T), 0) == iota((T, T), 1)
    return jnp.sum(jnp.where(eye, row, 0.0), axis=1, keepdims=True)


def doc_row(doc_ref, stretch):
    row = doc_ref[pl.ds(jnp.maximum(stretch, 0), 1), :].astype(F32)
    return jnp.where(stretch >= 0, row, -1.0)


def expand():
    return jnp.where(iota((32, W), 1) // 16 == iota((32, W), 0), 1.0, 0.0)


def fill_inverse(place_ref, inv_ref):
    for b in range(N):
        inv_ref[place_ref[b]] = b


def pack_kernel(q_ref, k_ref, v_ref, *outs):
    zq = lax.axis_index("seq") // 8
    for k, out in enumerate(outs):
        head = lax.rem(zq + k, 4)
        lanes = pl.ds(pl.multiple_of(head * HD, HD), HD)
        for t, ref in enumerate((q_ref, k_ref, v_ref)):
            out[t] = ref[:, lanes]


def local_kernel(place_ref, doc_ref, st_ref, se_ref, p_ref, f0_ref, g_ref, h_ref, x_ref):
    c = place_ref[lax.axis_index("seq")]
    row = doc_row(doc_ref, c)
    col = column(row)
    earlier = (row == col) & (iota((T, T), 1) < iota((T, T), 0))
    run = jnp.broadcast_to(jnp.sum(jnp.where(earlier, 1.0, 0.0), axis=1, keepdims=True), (T, T))
    ex = expand()
    x_ref[:, 0:8, :] = jnp.zeros((3, 8, W), F32)
    x_ref[:, 8:, :] = st_ref[...]
    taps = [jnp.dot(se_ref[j], ex, precision=HIGHEST, preferred_element_type=F32) for j in range(3)]
    for lane in range(4):
        ls = slice(lane * 128, lane * 128 + 128)
        feats = []
        for j in range(3):
            acc = x_ref[j, 8:, ls] * taps[j][0:1, ls]
            for lag in range(1, SE):
                acc = acc + jnp.where(
                    run >= lag, x_ref[j, 8 - lag : 8 + T - lag, ls] * taps[j][lag : lag + 1, ls], 0.0
                )
            feats.append(acc)
        f0_ref[:, ls] = feats[0]
        gated = feats[1] * feats[2]
        g_ref[:, ls] = gated
        for r in range(15):
            p_ref[r * 4 + lane] = gated[8 * r + 8 : 8 * r + 16]
        for j in (1, 2):
            h_ref[j - 1, :, ls] = feats[j][0:8]
            p_ref[(14 + j) * 4 + lane] = feats[j][0:8]
            p_ref[77 + j * 4 + lane] = st_ref[j, T - 8 :, ls]
        for j in range(3):
            p_ref[(17 + j) * 4 + lane] = st_ref[j, T - 8 :, ls]
    p_ref[80] = jnp.zeros((8, 128), F32)
    p_ref[89:96] = jnp.zeros((7, 8, 128), F32)


def select_kernel(place_ref, r_ref, s_ref, inv_ref):
    fill_inverse(place_ref, inv_ref)
    back = jnp.where(lax.axis_index("seq") < FAR, 1, 2)
    for d in range(N):
        s_ref[d] = r_ref[inv_ref[jnp.maximum(place_ref[d] - back, 0)]]


def halo(tail, taps, run):
    acc = jnp.zeros_like(tail)
    rows = iota(tail.shape, 0)
    for lag in range(1, SE):
        linked = (rows < lag) & (run >= lag)
        acc = acc + jnp.where(linked, pltpu.roll(tail, lag, 0) * taps[lag : lag + 1], 0.0)
    return acc


def hyena_kernel(place_ref, doc_ref, se_ref, mr_ref, decay_ref, f0_ref, g_ref, h_ref, p_ref, out_ref, e_ref, s_ref, t_ref):
    c = place_ref[lax.axis_index("seq")]
    row, before, before2 = (doc_row(doc_ref, c - i) for i in range(3))

    def run_of(rows, own, prev):
        same = jnp.sum(jnp.where(prev == rows, 1.0, 0.0), axis=1, keepdims=True)
        at = iota((rows.shape[0], T), 0)
        earlier = (own == rows) & (iota((rows.shape[0], T), 1) < at)
        return same + jnp.sum(jnp.where(earlier, 1.0, 0.0), axis=1, keepdims=True)

    run = jnp.broadcast_to(run_of(column(row), row, before), (T, T))
    run8 = jnp.broadcast_to(run[0:8, 0:1], (8, W))
    prev8 = jnp.broadcast_to(run_of(column(before)[0:8], before, before2), (8, W))
    ex = expand()
    lags = iota((32, T), 1).astype(F32)
    small = iota((32, 32), 0) == iota((32, 32), 1)
    decay = jnp.sum(jnp.where(small, decay_ref[...], 0.0), axis=1, keepdims=True)
    taps = mr_ref[...] * jnp.exp(-decay * lags)
    t_ref[...] = lax.dot_general(
        taps, ex, (((0,), (0,)), ((), ())), precision=HIGHEST, preferred_element_type=F32
    )
    short = [jnp.dot(se_ref[j], ex, precision=HIGHEST, preferred_element_type=F32) for j in range(3)]

    def rows_of(first):
        return jnp.concatenate([p_ref[first + lane] for lane in range(4)], axis=1)

    f0_head = f0_ref[0:8, :] + halo(rows_of(68), short[0], run8)
    own = [h_ref[j - 1] + halo(rows_of((17 + j) * 4), short[j], run8) for j in (1, 2)]
    prev = [rows_of((14 + j) * 4) + halo(rows_of(77 + j * 4), short[j], prev8) for j in (1, 2)]
    e_ref[0:8, :] = prev[0] * prev[1]
    for r in range(15):
        e_ref[8 * r + 8 : 8 * r + 16, :] = rows_of(r * 4)
    e_ref[T : T + 8, :] = own[0] * own[1]
    e_ref[T + 8 :, :] = g_ref[8:, :]
    for r in range(8):
        s_ref[r, 8:, :] = e_ref[8 - r : 256 - r, :]

    def lane_tile(lane, _):
        ls = pl.ds(pl.multiple_of(lane * 128, 128), 128)

        def eight(m, acc):
            rows = t_ref[pl.ds(pl.multiple_of(m * 8, 8), 8), ls]
            first = pl.multiple_of(T - m * 8, 8)
            for r in range(8):
                lag = (m * 8 + r).astype(F32)
                term = s_ref[r, pl.ds(first, T), ls] * rows[r : r + 1]
                acc = acc + jnp.where(run >= lag, term, 0.0)
            return acc

        acc = lax.fori_loop(0, 16, eight, jnp.zeros((T, 128), F32))
        out_ref[:, ls] = f0_ref[:, ls] * acc
        s_ref[0, 0:8, ls] = acc[0:8]
        return 0

    lax.fori_loop(0, 4, lane_tile, 0)
    out_ref[0:8, :] = f0_head * s_ref[0, 0:8, :]


def split(x):
    high = x.astype(jnp.bfloat16)
    return high, (x - high.astype(F32)).astype(jnp.bfloat16)


def dot3(a, b, dims):
    def dot(x, y):
        return lax.dot_general(x, y, (dims, ((), ())), preferred_element_type=F32)

    return dot(a[0], b[0]) + (dot(a[0], b[1]) + dot(a[1], b[0]))


def attend_kernel(
    place_ref, doc_ref, a0, a1, a2, a3, d_ref, cc, xx, cxx, zz, czz, d1, d2, cd1, cd2, *rest
):
    outs, (q_ref, kv_ref, inv_ref, kh, kl, vh, vl, s_ref, ph, pw, sem) = rest[:4], rest[4:]
    copies = []

    def fetch(src, dst):
        copy = pltpu.make_async_copy(src, dst, sem.at[len(copies)])
        copy.start()
        copies.append(copy)

    for i, ref in enumerate((a0, a1, a2, a3)):
        fetch(ref.at[0], q_ref.at[i])
    for x, ref in enumerate((d_ref, cc, xx, cxx, zz, czz)):
        fetch(ref, kv_ref.at[x])
    for x, (low, high) in ((6, (d1, d2)), (7, (cd1, cd2))):
        fetch(low, kv_ref.at[x, 0:4])
        fetch(high, kv_ref.at[x, 4:8])
    me = lax.axis_index("seq")
    zq, g = me // 8, lax.rem(me, 8)
    fill_inverse(place_ref, inv_ref)
    for copy in copies:
        copy.wait()
    scale = 1.0 / jnp.sqrt(jnp.float32(HD))
    causal = iota((T, T), 1) <= iota((T, T), 0)
    for i in range(4):
        c = place_ref[lax.rem(zq + 4 - i, 4) * 8 + g]
        col = column(doc_row(doc_ref, c))
        q = split(q_ref[i])
        keys = []
        for n in range(NB):
            at = c - (NB - 1) + n
            b = inv_ref[jnp.maximum(at, 0)]
            x = lax.bitwise_xor(lax.rem(b, 8), g)
            k = lax.rem(zq + 4 - b // 8, 4)
            rows = slice(n * T, n * T + T)
            kh[rows, :], kl[rows, :] = split(kv_ref[x, k])
            vh[rows, :], vl[rows, :] = split(kv_ref[x, k + 4])
            keys.append(doc_row(doc_ref, at))
        s_ref[...] = dot3(q, (kh[...], kl[...]), ((1,), (1,))) * scale
        top = None
        for n in range(NB):
            cols = slice(n * T, n * T + T)
            allowed = keys[n] == col
            if n == NB - 1:
                allowed = allowed & causal
            s = jnp.where(allowed, s_ref[:, cols], -1e30)
            s_ref[:, cols] = s
            top = s if top is None else jnp.maximum(top, s)
        top = jnp.max(top, axis=1, keepdims=True)
        total = jnp.zeros((T, T), F32)
        for n in range(NB):
            cols = slice(n * T, n * T + T)
            p = jnp.exp(s_ref[:, cols] - top)
            total = total + p
            ph[:, cols], pw[:, cols] = split(p)
        acc = dot3((ph[...], pw[...]), (vh[...], vl[...]), ((1,), (0,)))
        outs[i][...] = acc / jnp.sum(total, axis=1, keepdims=True)


def join_kernel(hy_ref, a0, a1, a2, a3, out_ref, sq_ref):
    zq = lax.axis_index("seq") // 8
    for k, ref in enumerate((a0, a1, a2, a3)):
        lanes = pl.ds(pl.multiple_of(lax.rem(zq + k, 4) * HD, HD), HD)
        out_ref[:, lanes] = hy_ref[:, lanes] + ref[...]
    y = out_ref[...]
    sq_ref[...] = lax.dot_general(
        jnp.ones((8, W), F32), y * y, (((1,), (1,)), ((), ())), precision=HIGHEST, preferred_element_type=F32
    )


def norm_kernel(y_ref, sq_ref, gain_ref, out_ref):
    mean = column(sq_ref[0:1, :]) / (8.0 * W)
    out_ref[...] = y_ref[...] * lax.rsqrt(mean + 1e-05) * gain_ref[...]


def call(kernel, out, ins, scratch=(), name=None):
    shapes = [jax.ShapeDtypeStruct(s, F32) for s in out]
    one = len(shapes) == 1
    return pl.pallas_call(
        kernel,
        out_shape=shapes[0] if one else shapes,
        in_specs=ins,
        out_specs=VMEM if one else [VMEM] * len(shapes),
        scratch_shapes=scratch,
        name=name,
    )


def per_device(streams, se_filter, mr_filter, mr_decay, query, key, value, placement_list, doc_ids, norm_gain):
    st = streams.transpose(1, 0, 2)
    se = se_filter.transpose(1, 0, 2)
    mr = mr_filter.T
    docs = doc_ids.reshape(N, T)

    def ring(x, k):
        return lax.ppermute(x, "seq", [(b, (b + 8 * k) % N) for b in range(N)])

    def swap(x, bit):
        return lax.ppermute(x, "seq", [(b, b ^ bit) for b in range(N)])

    mine = call(pack_kernel, [(3, T, HD)] * 4, [VMEM] * 3, name="pack")(query, key, value)
    held = [mine[0]] + [ring(mine[k], k) for k in (2, 1, 3)]
    held = [held[0], held[2], held[1], held[3]]

    tiles, f0, gated, heads = call(
        local_kernel,
        [(96, 8, 128), (T, W), (T, W), (2, 8, W)],
        [SMEM, VMEM, VMEM, VMEM],
        [pltpu.VMEM((3, T + 8, W), F32)],
        name="local",
    )(placement_list, docs, st, se)
    pieces = lax.all_to_all(tiles.reshape(N, 24, 128), "seq", 0, 0, tiled=True)

    kv = jnp.concatenate([a[t : t + 1] for t in (1, 2) for a in held], axis=0)
    xx, zz, cc = swap(kv, 2), swap(kv, 4), swap(kv, 1)
    d1, d2 = swap(zz[:4], 2), swap(xx[4:], 4)
    cxx, czz, cd1, cd2 = swap(xx, 1), swap(zz, 1), swap(d1, 1), swap(d2, 1)

    chosen = call(select_kernel, [(N, 24, 128)], [SMEM, VMEM], [pltpu.SMEM((N,), jnp.int32)], name="select")(
        placement_list, pieces
    )
    back = lax.all_to_all(chosen, "seq", 0, 0, tiled=True).reshape(96, 8, 128)
    hyena = call(
        hyena_kernel,
        [(T, W)],
        [SMEM] + [VMEM] * 8,
        [pltpu.VMEM((256, W), F32), pltpu.VMEM((8, 256, W), F32), pltpu.VMEM((T, W), F32)],
        name="hyena",
    )(placement_list, docs, se, mr, mr_decay.reshape(1, 32), f0, gated, heads, back)

    bf = jnp.bfloat16
    attended = call(
        attend_kernel,
        [(T, HD)] * 4,
        [SMEM, VMEM] + [ANY] * 14,
        [
            pltpu.VMEM((4, T, HD), F32),
            pltpu.VMEM((8, 8, T, HD), F32),
            pltpu.SMEM((N,), jnp.int32),
            pltpu.VMEM((NB * T, HD), bf),
            pltpu.VMEM((NB * T, HD), bf),
            pltpu.VMEM((NB * T, HD), bf),
            pltpu.VMEM((NB * T, HD), bf),
            pltpu.VMEM((T, NB * T), F32),
            pltpu.VMEM((T, NB * T), bf),
            pltpu.VMEM((T, NB * T), bf),
            pltpu.SemaphoreType.DMA((14,)),
        ],
        name="attend",
    )(placement_list, docs, *held, kv, cc, xx, cxx, zz, czz, d1, d2, cd1, cd2)
    home = [attended[0]] + [ring(attended[k], -k) for k in (2, 1, 3)]
    home = [home[0], home[2], home[1], home[3]]

    summed, squares = call(join_kernel, [(T, W), (8, 128)], [VMEM] * 5, name="join")(hyena, *home)
    for bit in (4, 2, 1):
        squares = squares + lax.ppermute(squares, "mp", [(b, b ^ bit) for b in range(8)])
    return call(norm_kernel, [(T, W)], [VMEM] * 3, name="norm")(summed, squares, norm_gain.reshape(1, W))


def solution(mesh):
    placed = (
        P("seq", None, "mp"),
        P(None, None, "mp"),
        P(None, "mp"),
        P("mp"),
        P("seq", "mp"),
        P("seq", "mp"),
        P("seq", "mp"),
        P(),
        P(),
        P("mp"),
    )
    return jax.shard_map(
        per_device, mesh=mesh, in_specs=placed, out_specs=P("seq", "mp"), check_vma=False
    )
```

```python
import jax
import jax.numpy as jnp
from jax import lax
from jax.experimental import pallas as pl
from jax.experimental.pallas import tpu as pltpu
from jax.sharding import PartitionSpec as P


N = 32
T = 128
HD = 128
W = 512
NB = 9
SE = 7
FAR = 27
VMEM = pl.BlockSpec(memory_space=pltpu.VMEM)
SMEM = pl.BlockSpec(memory_space=pltpu.SMEM)
ANY = pl.BlockSpec(memory_space=pl.ANY)
HIGHEST = lax.Precision.HIGHEST
F32 = jnp.float32


def hbm(x):
    return pltpu.with_memory_space_constraint(x, pltpu.HBM)


def vmem(x):
    return pltpu.with_memory_space_constraint(x, pltpu.VMEM)


def iota(shape, dim):
    return lax.broadcasted_iota(jnp.int32, shape, dim)


def column(row):
    eye = iota((T, T), 0) == iota((T, T), 1)
    return jnp.sum(jnp.where(eye, row, 0.0), axis=1, keepdims=True)


def doc_row(doc_ref, stretch):
    row = doc_ref[pl.ds(jnp.maximum(stretch, 0), 1), :].astype(F32)
    return jnp.where(stretch >= 0, row, -1.0)


def expand():
    return jnp.where(iota((32, W), 1) // 16 == iota((32, W), 0), 1.0, 0.0)


def fill_inverse(place_ref, inv_ref):
    for b in range(N):
        inv_ref[place_ref[b]] = b


def pack_kernel(q_ref, k_ref, v_ref, *outs):
    zq = lax.axis_index("seq") // 8
    for k, out in enumerate(outs):
        head = lax.rem(zq + k, 4)
        lanes = pl.ds(pl.multiple_of(head * HD, HD), HD)
        for t, ref in enumerate((q_ref, k_ref, v_ref)):
            out[t] = ref[:, lanes]


def local_kernel(place_ref, doc_ref, st_ref, se_ref, p_ref, f0_ref, g_ref, h_ref, short_ref, x_ref):
    c = place_ref[lax.axis_index("seq")]
    row = doc_row(doc_ref, c)
    col = column(row)
    earlier = (row == col) & (iota((T, T), 1) < iota((T, T), 0))
    run = jnp.broadcast_to(jnp.sum(jnp.where(earlier, 1.0, 0.0), axis=1, keepdims=True), (T, T))
    ex = expand()
    x_ref[:, 0:8, :] = jnp.zeros((3, 8, W), F32)
    x_ref[:, 8:, :] = st_ref[...]
    taps = [jnp.dot(se_ref[j], ex, precision=HIGHEST, preferred_element_type=F32) for j in range(3)]
    for j in range(3):
        short_ref[j] = taps[j]
    for lane in range(4):
        ls = slice(lane * 128, lane * 128 + 128)
        feats = []
        for j in range(3):
            acc = x_ref[j, 8:, ls] * taps[j][0:1, ls]
            for lag in range(1, SE):
                acc = acc + jnp.where(
                    run >= lag, x_ref[j, 8 - lag : 8 + T - lag, ls] * taps[j][lag : lag + 1, ls], 0.0
                )
            feats.append(acc)
        f0_ref[:, ls] = feats[0]
        gated = feats[1] * feats[2]
        g_ref[:, ls] = gated
        for r in range(15):
            p_ref[r * 4 + lane] = gated[8 * r + 8 : 8 * r + 16]
        for j in (1, 2):
            h_ref[j - 1, :, ls] = feats[j][0:8]
            p_ref[(14 + j) * 4 + lane] = feats[j][0:8]
            p_ref[77 + j * 4 + lane] = st_ref[j, T - 8 :, ls]
        for j in range(3):
            p_ref[(17 + j) * 4 + lane] = st_ref[j, T - 8 :, ls]
    p_ref[80] = jnp.zeros((8, 128), F32)
    p_ref[89:96] = jnp.zeros((7, 8, 128), F32)


def select_kernel(place_ref, r_ref, s_ref, inv_ref):
    fill_inverse(place_ref, inv_ref)
    back = jnp.where(lax.axis_index("seq") < FAR, 1, 2)
    for d in range(N):
        s_ref[d] = r_ref[inv_ref[jnp.maximum(place_ref[d] - back, 0)]]


def halo(tail, taps, run):
    acc = jnp.zeros_like(tail)
    rows = iota(tail.shape, 0)
    for lag in range(1, SE):
        linked = (rows < lag) & (run >= lag)
        acc = acc + jnp.where(linked, pltpu.roll(tail, lag, 0) * taps[lag : lag + 1], 0.0)
    return acc


def long_taps(mr_ref, decay_ref, ex):
    small = iota((32, 32), 0) == iota((32, 32), 1)
    decay = jnp.sum(jnp.where(small, decay_ref[...], 0.0), axis=1, keepdims=True)
    taps = mr_ref[...] * jnp.exp(-decay * iota((32, T), 1).astype(F32))
    return lax.dot_general(taps, ex, (((0,), (0,)), ((), ())), precision=HIGHEST, preferred_element_type=F32)


def run_of(rows, own, prev):
    same = jnp.sum(jnp.where(prev == rows, 1.0, 0.0), axis=1, keepdims=True)
    at = iota((rows.shape[0], T), 0)
    earlier = (own == rows) & (iota((rows.shape[0], T), 1) < at)
    return same + jnp.sum(jnp.where(earlier, 1.0, 0.0), axis=1, keepdims=True)


def convolve(e_ref, s_ref, t_ref, run_ref, span, plain, masked, keep, write):
    for r in range(8):
        s_ref[r, span[0] : span[1], :] = e_ref[span[0] - r : span[1] - r, :]

    def lane_tile(lane, _):
        ls = pl.ds(pl.multiple_of(lane * 128, 128), 128)
        acc = [jnp.zeros((8, 128), F32) for _ in range(16)]

        def terms(blocks, mask):
            for m in range(16):
                if not len(blocks(m)):
                    continue
                rows = t_ref[8 * m : 8 * m + 8, ls]
                for r in range(8):
                    tap = jnp.broadcast_to(rows[r : r + 1], (8, 128))
                    for i in blocks(m):
                        first = T - 8 * m + 8 * i
                        term = s_ref[r, first : first + 8, ls] * tap
                        if mask:
                            term = jnp.where(run_ref[8 * i : 8 * i + 8, :] >= 8 * m + r, term, 0.0)
                        acc[i] = acc[i] + term

        if keep is not None:
            terms(plain, False)
            for i in range(16):
                acc[i] = jnp.where(keep(i), acc[i], 0.0)
        terms(masked, True)
        write(ls, acc)
        return 0

    lax.fori_loop(0, 4, lane_tile, 0)


def own_kernel(place_ref, doc_ref, mr_ref, decay_ref, g_ref, out_ref, t_ref, e_ref, s_ref, run_ref):
    c = place_ref[lax.axis_index("seq")]
    row = doc_row(doc_ref, c)
    run_ref[...] = jnp.broadcast_to(run_of(column(row), row, doc_row(doc_ref, c - 1)), (T, T))
    t_ref[...] = long_taps(mr_ref, decay_ref, expand())
    e_ref[T : T + 8, :] = jnp.zeros((8, W), F32)
    e_ref[T + 8 :, :] = g_ref[8:, :]

    def write(ls, acc):
        for i in range(16):
            out_ref[8 * i : 8 * i + 8, ls] = acc[i]

    convolve(e_ref, s_ref, t_ref, run_ref, (T + 8, 2 * T), None, lambda m: range(m + 1, 16), None, write)


def halo_kernel(
    place_ref, doc_ref, short_ref, t_ref, f0_ref, own_ref, h_ref, p_ref, out_ref, e_ref, s_ref, run_ref, first_ref
):
    c = place_ref[lax.axis_index("seq")]
    row, before, before2 = (doc_row(doc_ref, c - i) for i in range(3))
    run = jnp.broadcast_to(run_of(column(row), row, before), (T, T))
    run_ref[...] = run
    run8 = jnp.broadcast_to(run[0:8, 0:1], (8, W))
    prev8 = jnp.broadcast_to(run_of(column(before)[0:8], before, before2), (8, W))
    short = [short_ref[j] for j in range(3)]
    start = row[:, 0:1]
    first_ref[...] = jnp.broadcast_to(jnp.where(column(row) == start, 1.0, 0.0), (T, T))
    linked = jnp.where(column(before) == start, 1.0, 0.0)

    def rows_of(first):
        return jnp.concatenate([p_ref[first + lane] for lane in range(4)], axis=1)

    own = [h_ref[j - 1] + halo(rows_of((17 + j) * 4), short[j], run8) for j in (1, 2)]
    prev = [rows_of((14 + j) * 4) + halo(rows_of(77 + j * 4), short[j], prev8) for j in (1, 2)]
    e_ref[0:8, :] = jnp.where(linked[0:8] > 0.0, prev[0] * prev[1], 0.0)
    for r in range(15):
        rows = slice(8 * r + 8, 8 * r + 16)
        e_ref[rows, :] = jnp.where(linked[rows] > 0.0, rows_of(r * 4), 0.0)
    e_ref[T : T + 8, :] = own[0] * own[1]
    e_ref[T + 8 : T + 16, :] = jnp.zeros((8, W), F32)
    out_ref[0:8, :] = f0_ref[0:8, :] + halo(rows_of(68), short[0], run8)
    out_ref[8:, :] = f0_ref[8:, :]

    def write(ls, acc):
        for i in range(16):
            rows = slice(8 * i, 8 * i + 8)
            out_ref[rows, ls] = out_ref[rows, ls] * (own_ref[rows, ls] + acc[i])

    def keep(i):
        return first_ref[8 * i : 8 * i + 8, :] > 0.0

    convolve(
        e_ref, s_ref, t_ref, run_ref, (8, T + 16), lambda m: range(0, m), lambda m: range(m, min(16, m + 2)), keep, write
    )


def split(x):
    high = x.astype(jnp.bfloat16)
    return high, (x - high.astype(F32)).astype(jnp.bfloat16)


def dot3(a, high, low, dims):
    def dot(x, y):
        return lax.dot_general(x, y, (dims, ((), ())), preferred_element_type=F32)

    both = dot(a, high)
    return both[:T] + (both[T:] + dot(a[:T], low))


def attend_kernel(
    place_ref, doc_ref, a0, a1, a2, a3, *rest
):
    kv, rest = rest[:16], rest[16:]
    outs, (q_ref, kv_ref, sem, kh, kl, vh, vl, s_ref, qs_ref, p_ref) = rest[:4], rest[4:]
    copies = []

    def fetch(src, dst):
        copies.append(pltpu.make_async_copy(src, dst, sem.at[len(copies)]))
        copies[-1].start()

    for n, ref in enumerate(kv):
        fetch(ref, kv_ref.at[n // 2, n % 2])
    for i, ref in enumerate((a0, a1, a2, a3)):
        fetch(ref.at[0], q_ref.at[i])
    me = lax.axis_index("seq")
    zq = me // 8
    g = lax.rem(me, 8)

    for x in range(8):
        copies[2 * x].wait()
        copies[2 * x + 1].wait()
        for k in range(4):
            at = place_ref[lax.rem(zq + 4 - k, 4) * 8 + lax.bitwise_xor(g, x)]
            rows = pl.ds(pl.multiple_of(at * T, T), T)
            kh[rows, :], kl[rows, :] = split(kv_ref[x, 0, k])
            vh[rows, :], vl[rows, :] = split(kv_ref[x, 1, k])
    for copy in copies[16:]:
        copy.wait()
    scale = 1.0 / jnp.sqrt(jnp.float32(HD))
    ahead = iota((T, T), 1) - iota((T, T), 0)
    for i in range(4):
        c = place_ref[lax.rem(zq + 4 - i, 4) * 8 + g]
        first = jnp.maximum(c - (NB - 1), 0)
        col = column(doc_row(doc_ref, c))
        qs_ref[:T, :], qs_ref[T:, :] = split(q_ref[i])
        rows = pl.ds(pl.multiple_of(first * T, T), NB * T)
        s_ref[...] = dot3(qs_ref[...], kh[rows, :], kl[rows, :], ((1,), (1,))) * scale
        top = None
        for n in range(NB):
            cols = slice(n * T, n * T + T)
            allowed = (doc_row(doc_ref, first + n) == col) & (ahead <= (c - first - n) * T)
            s = jnp.where(allowed, s_ref[:, cols], -1e30)
            s_ref[:, cols] = s
            top = s if top is None else jnp.maximum(top, s)
        top = jnp.max(top, axis=1, keepdims=True)
        total = jnp.zeros((T, T), F32)
        for n in range(NB):
            cols = slice(n * T, n * T + T)
            p = jnp.exp(s_ref[:, cols] - top)
            total = total + p
            p_ref[:T, cols], p_ref[T:, cols] = split(p)
        acc = dot3(p_ref[...], vh[rows, :], vl[rows, :], ((1,), (0,)))
        outs[i][...] = acc / jnp.sum(total, axis=1, keepdims=True)


def join_kernel(hy_ref, a0, a1, a2, a3, out_ref, sq_ref):
    zq = lax.axis_index("seq") // 8
    for k, ref in enumerate((a0, a1, a2, a3)):
        lanes = pl.ds(pl.multiple_of(lax.rem(zq + k, 4) * HD, HD), HD)
        out_ref[:, lanes] = hy_ref[:, lanes] + ref[...]
    y = out_ref[...]
    sq_ref[...] = lax.dot_general(
        jnp.ones((8, W), F32), y * y, (((1,), (1,)), ((), ())), precision=HIGHEST, preferred_element_type=F32
    )


def norm_kernel(y_ref, sq_ref, other_ref, gain_ref, out_ref):
    mean = column(sq_ref[0:1, :] + other_ref[0:1, :]) / (8.0 * W)
    out_ref[...] = y_ref[...] * lax.rsqrt(mean + 1e-05) * gain_ref[...]


def call(kernel, out, ins, scratch=()):
    shapes = [jax.ShapeDtypeStruct(s, F32) for s in out]
    one = len(shapes) == 1
    return pl.pallas_call(
        kernel,
        out_shape=shapes[0] if one else shapes,
        in_specs=ins,
        out_specs=VMEM if one else [VMEM] * len(shapes),
        scratch_shapes=scratch,
    )


def per_device(streams, se_filter, mr_filter, mr_decay, query, key, value, placement_list, doc_ids, norm_gain):
    st = streams.transpose(1, 0, 2)
    se = se_filter.transpose(1, 0, 2)
    mr = mr_filter.T
    docs = doc_ids.reshape(N, T)

    def ring(x, k):
        return lax.ppermute(x, "seq", [(b, (b + 8 * k) % N) for b in range(N)])

    def swap(x, axis, bit):
        return lax.ppermute(x, axis, [(b, b ^ bit) for b in range(N if axis == "seq" else 8)])

    packed = call(pack_kernel, [(3, T, HD)] * 4, [VMEM] * 3)(query, key, value)
    held = [packed[0]] + [None] * 3
    for k in (2, 1, 3):
        held[k] = ring(packed[k], k)

    tiles, f0, gated, heads, short = call(
        local_kernel,
        [(96, 8, 128), (T, W), (T, W), (2, 8, W), (3, SE, W)],
        [SMEM, VMEM, VMEM, VMEM],
        [pltpu.VMEM((3, T + 8, W), F32)],
    )(placement_list, docs, st, se)
    pieces = lax.all_to_all(tiles.reshape(N, 24, 128), "seq", 0, 0, tiled=True)
    conv = [pltpu.VMEM((256, W), F32), pltpu.VMEM((8, 256, W), F32), pltpu.VMEM((T, T), F32)]
    decay = mr_decay.reshape(1, 32)
    own, taps = call(own_kernel, [(T, W), (T, W)], [SMEM] + [VMEM] * 4, conv)(placement_list, docs, mr, decay, gated)

    k0, v0 = (jnp.concatenate([a[t : t + 1] for a in held], axis=0) for t in (1, 2))
    zk = swap(k0, "seq", 4)
    xv = swap(v0, "seq", 2)
    zv = swap(v0, "seq", 4)
    xk = swap(k0, "seq", 2)
    dk = swap(zk, "seq", 2)
    dv = swap(xv, "seq", 4)
    ck, cv, cxk, cxv, czk, czv, cdk, cdv = (
        swap(a, "seq", 1) for a in (k0, v0, xk, xv, zk, zv, dk, dv)
    )

    chosen = call(select_kernel, [(N, 24, 128)], [SMEM, VMEM], [pltpu.SMEM((N,), jnp.int32)])(
        placement_list, hbm(pieces)
    )
    back = lax.all_to_all(chosen, "seq", 0, 0, tiled=True).reshape(96, 8, 128)

    bf = jnp.bfloat16
    pieces_kv = (k0, v0, ck, cv, xk, xv, cxk, cxv, zk, zv, czk, czv, dk, dv, cdk, cdv)
    near = [hbm(a) for a in (*held[1:], *pieces_kv)]
    attended = call(
        attend_kernel,
        [(T, HD)] * 4,
        [SMEM, VMEM] + [ANY] * 20,
        [
            pltpu.VMEM((4, T, HD), F32),
            pltpu.VMEM((8, 2, 4, T, HD), F32),
            pltpu.SemaphoreType.DMA((20,)),
            *[pltpu.VMEM((N * T, HD), bf)] * 4,
            pltpu.VMEM((T, NB * T), F32),
            pltpu.VMEM((2 * T, HD), bf),
            pltpu.VMEM((2 * T, NB * T), bf),
        ],
    )(placement_list, docs, held[0], *near)
    home = [attended[0]] + [None] * 3
    for k in (2, 1, 3):
        home[k] = ring(attended[k], -k)

    hyena = call(halo_kernel, [(T, W)], [SMEM] + [VMEM] * 7, [*conv, pltpu.VMEM((T, T), F32)])(
        placement_list, docs, short, taps, f0, own, heads, vmem(back)
    )
    summed, squares = call(join_kernel, [(T, W), (8, 128)], [VMEM] * 5)(hyena, home[0], *map(vmem, home[1:]))

    def along_y(k):
        return lax.ppermute(squares, "mp", [(m, (m + 2 * k) % 8) for m in range(8)])

    squares = squares + along_y(2) + (along_y(1) + along_y(3))
    other = swap(squares, "mp", 1)
    return call(norm_kernel, [(T, W)], [VMEM] * 4)(summed, squares, vmem(other), norm_gain.reshape(1, W))


def solution(mesh):
    placed = (
        P("seq", None, "mp"),
        P(None, None, "mp"),
        P(None, "mp"),
        P("mp"),
        P("seq", "mp"),
        P("seq", "mp"),
        P("seq", "mp"),
        P(),
        P(),
        P("mp"),
    )
    return jax.shard_map(per_device, mesh=mesh, in_specs=placed, out_specs=P("seq", "mp"), check_vma=False)
```

```python
import jax
import jax.numpy as jnp
from jax import lax
from jax.experimental import pallas as pl
from jax.experimental.pallas import tpu as pltpu
from jax.sharding import PartitionSpec as P


N = 32
T = 128
HD = 128
W = 512
NB = 9
SE = 7
FAR = 27
VMEM = pl.BlockSpec(memory_space=pltpu.VMEM)
SMEM = pl.BlockSpec(memory_space=pltpu.SMEM)
ANY = pl.BlockSpec(memory_space=pl.ANY)
HIGHEST = lax.Precision.HIGHEST
F32 = jnp.float32


def hbm(x):
    return pltpu.with_memory_space_constraint(x, pltpu.HBM)


def vmem(x):
    return pltpu.with_memory_space_constraint(x, pltpu.VMEM)


def iota(shape, dim):
    return lax.broadcasted_iota(jnp.int32, shape, dim)


def column(row):
    eye = iota((T, T), 0) == iota((T, T), 1)
    return jnp.sum(jnp.where(eye, row, 0.0), axis=1, keepdims=True)


def doc_row(doc_ref, stretch):
    row = doc_ref[pl.ds(jnp.maximum(stretch, 0), 1), :].astype(F32)
    return jnp.where(stretch >= 0, row, -1.0)


def expand():
    return jnp.where(iota((32, W), 1) // 16 == iota((32, W), 0), 1.0, 0.0)


def fill_inverse(place_ref, inv_ref):
    for b in range(N):
        inv_ref[place_ref[b]] = b


def pack_kernel(q_ref, k_ref, v_ref, *outs):
    zq = lax.axis_index("seq") // 8
    for k, out in enumerate(outs):
        head = lax.rem(zq + k, 4)
        lanes = pl.ds(pl.multiple_of(head * HD, HD), HD)
        for t, ref in enumerate((q_ref, k_ref, v_ref)):
            out[t] = ref[:, lanes]


def local_kernel(place_ref, doc_ref, st_ref, se_ref, p_ref, f0_ref, g_ref, h_ref, short_ref, x_ref):
    c = place_ref[lax.axis_index("seq")]
    row = doc_row(doc_ref, c)
    col = column(row)
    earlier = (row == col) & (iota((T, T), 1) < iota((T, T), 0))
    run = jnp.broadcast_to(jnp.sum(jnp.where(earlier, 1.0, 0.0), axis=1, keepdims=True), (T, T))
    ex = expand()
    x_ref[:, 0:8, :] = jnp.zeros((3, 8, W), F32)
    x_ref[:, 8:, :] = st_ref[...]
    taps = [jnp.dot(se_ref[j], ex, precision=HIGHEST, preferred_element_type=F32) for j in range(3)]
    for j in range(3):
        short_ref[j] = taps[j]
    for lane in range(4):
        ls = slice(lane * 128, lane * 128 + 128)
        feats = []
        for j in range(3):
            acc = x_ref[j, 8:, ls] * taps[j][0:1, ls]
            for lag in range(1, SE):
                acc = acc + jnp.where(
                    run >= lag, x_ref[j, 8 - lag : 8 + T - lag, ls] * taps[j][lag : lag + 1, ls], 0.0
                )
            feats.append(acc)
        f0_ref[:, ls] = feats[0]
        gated = feats[1] * feats[2]
        g_ref[:, ls] = gated
        for r in range(15):
            p_ref[r * 4 + lane] = gated[8 * r + 8 : 8 * r + 16]
        for j in (1, 2):
            h_ref[j - 1, :, ls] = feats[j][0:8]
            p_ref[(14 + j) * 4 + lane] = feats[j][0:8]
            p_ref[77 + j * 4 + lane] = st_ref[j, T - 8 :, ls]
        for j in range(3):
            p_ref[(17 + j) * 4 + lane] = st_ref[j, T - 8 :, ls]
    p_ref[80] = jnp.zeros((8, 128), F32)
    p_ref[89:96] = jnp.zeros((7, 8, 128), F32)


def select_kernel(place_ref, r_ref, s_ref, inv_ref):
    fill_inverse(place_ref, inv_ref)
    back = jnp.where(lax.axis_index("seq") < FAR, 1, 2)
    for d in range(N):
        s_ref[d] = r_ref[inv_ref[jnp.maximum(place_ref[d] - back, 0)]]


def halo(tail, taps, run):
    acc = jnp.zeros_like(tail)
    rows = iota(tail.shape, 0)
    for lag in range(1, SE):
        linked = (rows < lag) & (run >= lag)
        acc = acc + jnp.where(linked, pltpu.roll(tail, lag, 0) * taps[lag : lag + 1], 0.0)
    return acc


def long_taps(mr_ref, decay_ref, ex):
    small = iota((32, 32), 0) == iota((32, 32), 1)
    decay = jnp.sum(jnp.where(small, decay_ref[...], 0.0), axis=1, keepdims=True)
    taps = mr_ref[...] * jnp.exp(-decay * iota((32, T), 1).astype(F32))
    return lax.dot_general(taps, ex, (((0,), (0,)), ((), ())), precision=HIGHEST, preferred_element_type=F32)


def run_of(rows, own, prev):
    same = jnp.sum(jnp.where(prev == rows, 1.0, 0.0), axis=1, keepdims=True)
    at = iota((rows.shape[0], T), 0)
    earlier = (own == rows) & (iota((rows.shape[0], T), 1) < at)
    return same + jnp.sum(jnp.where(earlier, 1.0, 0.0), axis=1, keepdims=True)


def convolve(e_ref, s_ref, t_ref, run_ref, span, plain, masked, keep, write):
    for r in range(8):
        s_ref[r, span[0] : span[1], :] = e_ref[span[0] - r : span[1] - r, :]

    def lane_tile(lane, _):
        ls = pl.ds(pl.multiple_of(lane * 128, 128), 128)
        acc = [jnp.zeros((8, 128), F32) for _ in range(16)]

        def terms(blocks, mask):
            for m in range(16):
                if not len(blocks(m)):
                    continue
                rows = t_ref[8 * m : 8 * m + 8, ls]
                for r in range(8):
                    tap = jnp.broadcast_to(rows[r : r + 1], (8, 128))
                    for i in blocks(m):
                        first = T - 8 * m + 8 * i
                        term = s_ref[r, first : first + 8, ls] * tap
                        if mask:
                            term = jnp.where(run_ref[8 * i : 8 * i + 8, :] >= 8 * m + r, term, 0.0)
                        acc[i] = acc[i] + term

        if keep is not None:
            terms(plain, False)
            for i in range(16):
                acc[i] = jnp.where(keep(i), acc[i], 0.0)
        terms(masked, True)
        write(ls, acc)
        return 0

    lax.fori_loop(0, 4, lane_tile, 0)


def own_kernel(place_ref, doc_ref, mr_ref, decay_ref, g_ref, out_ref, t_ref, e_ref, s_ref, run_ref):
    c = place_ref[lax.axis_index("seq")]
    row = doc_row(doc_ref, c)
    run_ref[...] = jnp.broadcast_to(run_of(column(row), row, doc_row(doc_ref, c - 1)), (T, T))
    t_ref[...] = long_taps(mr_ref, decay_ref, expand())
    e_ref[T : T + 8, :] = jnp.zeros((8, W), F32)
    e_ref[T + 8 :, :] = g_ref[8:, :]

    def write(ls, acc):
        for i in range(16):
            out_ref[8 * i : 8 * i + 8, ls] = acc[i]

    convolve(e_ref, s_ref, t_ref, run_ref, (T + 8, 2 * T), None, lambda m: range(m + 1, 16), None, write)


def halo_kernel(
    place_ref, doc_ref, short_ref, t_ref, f0_ref, own_ref, h_ref, p_ref, out_ref, e_ref, s_ref, run_ref, first_ref
):
    c = place_ref[lax.axis_index("seq")]
    row, before, before2 = (doc_row(doc_ref, c - i) for i in range(3))
    run = jnp.broadcast_to(run_of(column(row), row, before), (T, T))
    run_ref[...] = run
    run8 = jnp.broadcast_to(run[0:8, 0:1], (8, W))
    prev8 = jnp.broadcast_to(run_of(column(before)[0:8], before, before2), (8, W))
    short = [short_ref[j] for j in range(3)]
    start = row[:, 0:1]
    first_ref[...] = jnp.broadcast_to(jnp.where(column(row) == start, 1.0, 0.0), (T, T))
    linked = jnp.where(column(before) == start, 1.0, 0.0)

    def rows_of(first):
        return jnp.concatenate([p_ref[first + lane] for lane in range(4)], axis=1)

    own = [h_ref[j - 1] + halo(rows_of((17 + j) * 4), short[j], run8) for j in (1, 2)]
    prev = [rows_of((14 + j) * 4) + halo(rows_of(77 + j * 4), short[j], prev8) for j in (1, 2)]
    e_ref[0:8, :] = jnp.where(linked[0:8] > 0.0, prev[0] * prev[1], 0.0)
    for r in range(15):
        rows = slice(8 * r + 8, 8 * r + 16)
        e_ref[rows, :] = jnp.where(linked[rows] > 0.0, rows_of(r * 4), 0.0)
    e_ref[T : T + 8, :] = own[0] * own[1]
    e_ref[T + 8 : T + 16, :] = jnp.zeros((8, W), F32)
    out_ref[0:8, :] = f0_ref[0:8, :] + halo(rows_of(68), short[0], run8)
    out_ref[8:, :] = f0_ref[8:, :]

    def write(ls, acc):
        for i in range(16):
            rows = slice(8 * i, 8 * i + 8)
            out_ref[rows, ls] = out_ref[rows, ls] * (own_ref[rows, ls] + acc[i])

    def keep(i):
        return first_ref[8 * i : 8 * i + 8, :] > 0.0

    convolve(
        e_ref, s_ref, t_ref, run_ref, (8, T + 16), lambda m: range(0, m), lambda m: range(m, min(16, m + 2)), keep, write
    )


def split(x):
    high = x.astype(jnp.bfloat16)
    return high, (x - high.astype(F32)).astype(jnp.bfloat16)


def dot(a, b, dims):
    return lax.dot_general(a, b, (dims, ((), ())), preferred_element_type=F32)


def attend_kernel(
    place_ref, doc_ref, a0, a1, a2, a3, *rest
):
    kv, late, rest = rest[:14], rest[14:16], rest[16:]
    outs, (q_ref, kv_ref, sem, k_ref, v_ref, s_ref, qs_ref, p_ref) = rest[:4], rest[4:]
    copies = []

    def fetch(src, dst):
        copies.append(pltpu.make_async_copy(src, dst, sem.at[len(copies)]))
        copies[-1].start()

    for n, ref in enumerate(kv):
        fetch(ref, kv_ref.at[n // 2, n % 2])
    for i, ref in enumerate((a0, a1, a2, a3)):
        fetch(ref.at[0], q_ref.at[i])
    me = lax.axis_index("seq")
    zq = me // 8
    g = lax.rem(me, 8)

    for x in range(8):
        if x < 7:
            copies[2 * x].wait()
            copies[2 * x + 1].wait()
        for k in range(4):
            at = place_ref[lax.rem(zq + 4 - k, 4) * 8 + lax.bitwise_xor(g, x)]
            rows = pl.ds(pl.multiple_of(at * T, T), T)
            k_ref[rows, :HD], k_ref[rows, HD:] = split(kv_ref[x, 0, k] if x < 7 else late[0][k])
            v_ref[rows, :HD], v_ref[rows, HD:] = split(kv_ref[x, 1, k] if x < 7 else late[1][k])
    for copy in copies[14:]:
        copy.wait()
    scale = 1.0 / jnp.sqrt(jnp.float32(HD))
    ahead = iota((T, T), 1) - iota((T, T), 0)
    home = [place_ref[lax.rem(zq + 4 - i, 4) * 8 + g] for i in range(4)]
    first = [jnp.maximum(c - (NB - 1), 0) for c in home]
    window = [pl.ds(pl.multiple_of(f * T, T), NB * T) for f in first]

    def score(i):
        high, low = split(q_ref[i])
        qs_ref[i, :T, :HD], qs_ref[i, :T, HD:] = high, high
        qs_ref[i, T:, :HD], qs_ref[i, T:, HD:] = low, jnp.zeros_like(low)
        both = dot(qs_ref[i], k_ref[window[i], :], ((1,), (1,)))
        s_ref[i % 2] = (both[:T] + both[T:]) * scale

    score(0)
    for i in range(4):
        if i < 3:
            score(i + 1)
        col = column(doc_row(doc_ref, home[i]))
        top = None
        for n in range(NB):
            cols = slice(n * T, n * T + T)
            allowed = (doc_row(doc_ref, first[i] + n) == col) & (ahead <= (home[i] - first[i] - n) * T)
            s = jnp.where(allowed, s_ref[i % 2, :, cols], -1e30)
            s_ref[i % 2, :, cols] = s
            top = s if top is None else jnp.maximum(top, s)
        top = jnp.max(top, axis=1, keepdims=True)
        total = jnp.zeros((T, T), F32)
        for n in range(NB):
            cols = slice(n * T, n * T + T)
            p = jnp.exp(s_ref[i % 2, :, cols] - top)
            total = total + p
            p_ref[i % 2, :T, cols], p_ref[i % 2, T:, cols] = split(p)
        acc = dot(p_ref[i % 2], v_ref[window[i], :], ((1,), (0,)))
        acc = acc[:T, :HD] + (acc[:T, HD:] + acc[T:, :HD])
        outs[i][...] = acc / jnp.sum(total, axis=1, keepdims=True)


def join_kernel(hy_ref, a0, a1, a2, a3, out_ref, sq_ref):
    zq = lax.axis_index("seq") // 8
    for k, ref in enumerate((a0, a1, a2, a3)):
        lanes = pl.ds(pl.multiple_of(lax.rem(zq + k, 4) * HD, HD), HD)
        out_ref[:, lanes] = hy_ref[:, lanes] + ref[...]
    y = out_ref[...]
    sq_ref[...] = lax.dot_general(
        jnp.ones((8, W), F32), y * y, (((1,), (1,)), ((), ())), precision=HIGHEST, preferred_element_type=F32
    )


def norm_kernel(y_ref, sq_ref, other_ref, gain_ref, out_ref):
    mean = column(sq_ref[0:1, :] + other_ref[0:1, :]) / (8.0 * W)
    out_ref[...] = y_ref[...] * lax.rsqrt(mean + 1e-05) * gain_ref[...]


def call(kernel, out, ins, scratch=()):
    shapes = [jax.ShapeDtypeStruct(s, F32) for s in out]
    one = len(shapes) == 1
    return pl.pallas_call(
        kernel,
        out_shape=shapes[0] if one else shapes,
        in_specs=ins,
        out_specs=VMEM if one else [VMEM] * len(shapes),
        scratch_shapes=scratch,
    )


def per_device(streams, se_filter, mr_filter, mr_decay, query, key, value, placement_list, doc_ids, norm_gain):
    st = streams.transpose(1, 0, 2)
    se = se_filter.transpose(1, 0, 2)
    mr = mr_filter.T
    docs = doc_ids.reshape(N, T)

    def ring(x, k):
        return lax.ppermute(x, "seq", [(b, (b + 8 * k) % N) for b in range(N)])

    def swap(x, axis, bit):
        return lax.ppermute(x, axis, [(b, b ^ bit) for b in range(N if axis == "seq" else 8)])

    packed = call(pack_kernel, [(3, T, HD)] * 4, [VMEM] * 3)(query, key, value)
    held = [packed[0]] + [None] * 3
    for k in (2, 1, 3):
        held[k] = ring(packed[k], k)

    tiles, f0, gated, heads, short = call(
        local_kernel,
        [(96, 8, 128), (T, W), (T, W), (2, 8, W), (3, SE, W)],
        [SMEM, VMEM, VMEM, VMEM],
        [pltpu.VMEM((3, T + 8, W), F32)],
    )(placement_list, docs, st, se)
    pieces = lax.all_to_all(tiles.reshape(N, 24, 128), "seq", 0, 0, tiled=True)
    conv = [pltpu.VMEM((256, W), F32), pltpu.VMEM((8, 256, W), F32), pltpu.VMEM((T, T), F32)]
    decay = mr_decay.reshape(1, 32)
    own, taps = call(own_kernel, [(T, W), (T, W)], [SMEM] + [VMEM] * 4, conv)(placement_list, docs, mr, decay, gated)

    k0, v0 = (jnp.concatenate([a[t : t + 1] for a in held], axis=0) for t in (1, 2))
    zk = swap(k0, "seq", 4)
    xv = swap(v0, "seq", 2)
    zv = swap(v0, "seq", 4)
    xk = swap(k0, "seq", 2)
    dk = swap(zk, "seq", 2)
    dv = swap(xv, "seq", 4)
    ck, cv = swap(k0, "seq", 1), swap(v0, "seq", 1)
    czk, cxv = swap(zk, "seq", 1), swap(xv, "seq", 1)
    czv, cxk = swap(zv, "seq", 1), swap(xk, "seq", 1)
    cdk, cdv = swap(dk, "seq", 1), swap(dv, "seq", 1)

    chosen = call(select_kernel, [(N, 24, 128)], [SMEM, VMEM], [pltpu.SMEM((N,), jnp.int32)])(
        placement_list, hbm(pieces)
    )
    back = lax.all_to_all(chosen, "seq", 0, 0, tiled=True).reshape(96, 8, 128)

    bf = jnp.bfloat16
    pieces_kv = (k0, v0, ck, cv, xk, xv, cxk, cxv, zk, zv, czk, czv, dk, dv, cdk, cdv)
    near = [hbm(a) for a in (*held[1:], *pieces_kv[:14])]
    near += [vmem(cdk), vmem(cdv)]
    attended = call(
        attend_kernel,
        [(T, HD)] * 4,
        [SMEM, VMEM] + [ANY] * 18 + [VMEM] * 2,
        [
            pltpu.VMEM((4, T, HD), F32),
            pltpu.VMEM((7, 2, 4, T, HD), F32),
            pltpu.SemaphoreType.DMA((18,)),
            *[pltpu.VMEM((N * T, 2 * HD), bf)] * 2,
            pltpu.VMEM((2, T, NB * T), F32),
            pltpu.VMEM((4, 2 * T, 2 * HD), bf),
            pltpu.VMEM((2, 2 * T, NB * T), bf),
        ],
    )(placement_list, docs, held[0], *near)
    home = [attended[0]] + [None] * 3
    for k in (2, 1, 3):
        home[k] = ring(attended[k], -k)

    hyena = call(halo_kernel, [(T, W)], [SMEM] + [VMEM] * 7, [*conv, pltpu.VMEM((T, T), F32)])(
        placement_list, docs, short, taps, f0, own, heads, vmem(back)
    )
    summed, squares = call(join_kernel, [(T, W), (8, 128)], [VMEM] * 5)(hyena, home[0], *map(vmem, home[1:]))

    def along_y(k):
        return lax.ppermute(squares, "mp", [(m, (m + 2 * k) % 8) for m in range(8)])

    squares = squares + along_y(2) + (along_y(1) + along_y(3))
    other = swap(squares, "mp", 1)
    return call(norm_kernel, [(T, W)], [VMEM] * 4)(summed, squares, vmem(other), norm_gain.reshape(1, W))


def solution(mesh):
    placed = (
        P("seq", None, "mp"),
        P(None, None, "mp"),
        P(None, "mp"),
        P("mp"),
        P("seq", "mp"),
        P("seq", "mp"),
        P("seq", "mp"),
        P(),
        P(),
        P("mp"),
    )
    return jax.shard_map(per_device, mesh=mesh, in_specs=placed, out_specs=P("seq", "mp"), check_vma=False)
```

```python
import jax
import jax.numpy as jnp
from jax import lax
from jax.experimental import pallas as pl
from jax.experimental.pallas import tpu as pltpu
from jax.sharding import PartitionSpec as P


N = 32
T = 128
HD = 128
W = 512
NB = 9
SE = 7
FAR = 27
VMEM = pl.BlockSpec(memory_space=pltpu.VMEM)
SMEM = pl.BlockSpec(memory_space=pltpu.SMEM)
ANY = pl.BlockSpec(memory_space=pl.ANY)
HIGHEST = lax.Precision.HIGHEST
F32 = jnp.float32


def hbm(x):
    return pltpu.with_memory_space_constraint(x, pltpu.HBM)


def vmem(x):
    return pltpu.with_memory_space_constraint(x, pltpu.VMEM)


def iota(shape, dim):
    return lax.broadcasted_iota(jnp.int32, shape, dim)


def column(row):
    eye = iota((T, T), 0) == iota((T, T), 1)
    return jnp.sum(jnp.where(eye, row, 0.0), axis=1, keepdims=True)


def doc_row(doc_ref, stretch):
    row = doc_ref[pl.ds(jnp.maximum(stretch, 0), 1), :].astype(F32)
    return jnp.where(stretch >= 0, row, -1.0)


def expand():
    return jnp.where(iota((32, W), 1) // 16 == iota((32, W), 0), 1.0, 0.0)


def fill_inverse(place_ref, inv_ref):
    for b in range(N):
        inv_ref[place_ref[b]] = b


def pack_kernel(q_ref, k_ref, v_ref, *outs):
    zq = lax.axis_index("seq") // 8
    for k, out in enumerate(outs):
        head = lax.rem(zq + k, 4)
        lanes = pl.ds(pl.multiple_of(head * HD, HD), HD)
        for t, ref in enumerate((q_ref, k_ref, v_ref)):
            out[t] = ref[:, lanes]


def local_kernel(place_ref, doc_ref, st_ref, se_ref, p_ref, f0_ref, g_ref, h_ref, short_ref, x_ref):
    c = place_ref[lax.axis_index("seq")]
    row = doc_row(doc_ref, c)
    col = column(row)
    earlier = (row == col) & (iota((T, T), 1) < iota((T, T), 0))
    run = jnp.broadcast_to(jnp.sum(jnp.where(earlier, 1.0, 0.0), axis=1, keepdims=True), (T, T))
    ex = expand()
    x_ref[:, 0:8, :] = jnp.zeros((3, 8, W), F32)
    x_ref[:, 8:, :] = st_ref[...]
    taps = [jnp.dot(se_ref[j], ex, precision=HIGHEST, preferred_element_type=F32) for j in range(3)]
    for j in range(3):
        short_ref[j] = taps[j]
    for lane in range(4):
        ls = slice(lane * 128, lane * 128 + 128)
        feats = []
        for j in range(3):
            acc = x_ref[j, 8:, ls] * taps[j][0:1, ls]
            for lag in range(1, SE):
                acc = acc + jnp.where(
                    run >= lag, x_ref[j, 8 - lag : 8 + T - lag, ls] * taps[j][lag : lag + 1, ls], 0.0
                )
            feats.append(acc)
        f0_ref[:, ls] = feats[0]
        gated = feats[1] * feats[2]
        g_ref[:, ls] = gated
        for r in range(15):
            p_ref[r * 4 + lane] = gated[8 * r + 8 : 8 * r + 16]
        for j in (1, 2):
            h_ref[j - 1, :, ls] = feats[j][0:8]
            p_ref[(14 + j) * 4 + lane] = feats[j][0:8]
            p_ref[77 + j * 4 + lane] = st_ref[j, T - 8 :, ls]
        for j in range(3):
            p_ref[(17 + j) * 4 + lane] = st_ref[j, T - 8 :, ls]
    p_ref[80] = jnp.zeros((8, 128), F32)
    p_ref[89:96] = jnp.zeros((7, 8, 128), F32)


def select_kernel(place_ref, r_ref, s_ref, inv_ref):
    fill_inverse(place_ref, inv_ref)
    back = jnp.where(lax.axis_index("seq") < FAR, 1, 2)
    for d in range(N):
        s_ref[d] = r_ref[inv_ref[jnp.maximum(place_ref[d] - back, 0)]]


def halo(tail, taps, run):
    acc = jnp.zeros_like(tail)
    rows = iota(tail.shape, 0)
    for lag in range(1, SE):
        linked = (rows < lag) & (run >= lag)
        acc = acc + jnp.where(linked, pltpu.roll(tail, lag, 0) * taps[lag : lag + 1], 0.0)
    return acc


def long_taps(mr_ref, decay_ref, ex):
    small = iota((32, 32), 0) == iota((32, 32), 1)
    decay = jnp.sum(jnp.where(small, decay_ref[...], 0.0), axis=1, keepdims=True)
    taps = mr_ref[...] * jnp.exp(-decay * iota((32, T), 1).astype(F32))
    return lax.dot_general(taps, ex, (((0,), (0,)), ((), ())), precision=HIGHEST, preferred_element_type=F32)


def run_of(rows, own, prev):
    same = jnp.sum(jnp.where(prev == rows, 1.0, 0.0), axis=1, keepdims=True)
    at = iota((rows.shape[0], T), 0)
    earlier = (own == rows) & (iota((rows.shape[0], T), 1) < at)
    return same + jnp.sum(jnp.where(earlier, 1.0, 0.0), axis=1, keepdims=True)


def convolve(e_ref, s_ref, t_ref, run_ref, span, plain, masked, keep, write):
    for r in range(8):
        s_ref[r, span[0] : span[1], :] = e_ref[span[0] - r : span[1] - r, :]

    def lane_tile(lane, _):
        ls = pl.ds(pl.multiple_of(lane * 128, 128), 128)
        acc = [jnp.zeros((8, 128), F32) for _ in range(16)]

        def terms(blocks, mask):
            for m in range(16):
                if not len(blocks(m)):
                    continue
                rows = t_ref[8 * m : 8 * m + 8, ls]
                for r in range(8):
                    tap = jnp.broadcast_to(rows[r : r + 1], (8, 128))
                    for i in blocks(m):
                        first = T - 8 * m + 8 * i
                        term = s_ref[r, first : first + 8, ls] * tap
                        if mask:
                            term = jnp.where(run_ref[8 * i : 8 * i + 8, :] >= 8 * m + r, term, 0.0)
                        acc[i] = acc[i] + term

        if keep is not None:
            terms(plain, False)
            for i in range(16):
                acc[i] = jnp.where(keep(i), acc[i], 0.0)
        terms(masked, True)
        write(ls, acc)
        return 0

    lax.fori_loop(0, 4, lane_tile, 0)


def own_kernel(place_ref, doc_ref, mr_ref, decay_ref, g_ref, out_ref, t_ref, e_ref, s_ref, run_ref):
    c = place_ref[lax.axis_index("seq")]
    row = doc_row(doc_ref, c)
    run_ref[...] = jnp.broadcast_to(run_of(column(row), row, doc_row(doc_ref, c - 1)), (T, T))
    t_ref[...] = long_taps(mr_ref, decay_ref, expand())
    e_ref[T : T + 8, :] = jnp.zeros((8, W), F32)
    e_ref[T + 8 :, :] = g_ref[8:, :]

    def write(ls, acc):
        for i in range(16):
            out_ref[8 * i : 8 * i + 8, ls] = acc[i]

    convolve(e_ref, s_ref, t_ref, run_ref, (T + 8, 2 * T), None, lambda m: range(m + 1, 16), None, write)


def halo_kernel(
    place_ref, doc_ref, short_ref, t_ref, f0_ref, own_ref, h_ref, p_ref, out_ref, e_ref, s_ref, run_ref, first_ref
):
    c = place_ref[lax.axis_index("seq")]
    row, before, before2 = (doc_row(doc_ref, c - i) for i in range(3))
    run = jnp.broadcast_to(run_of(column(row), row, before), (T, T))
    run_ref[...] = run
    run8 = jnp.broadcast_to(run[0:8, 0:1], (8, W))
    prev8 = jnp.broadcast_to(run_of(column(before)[0:8], before, before2), (8, W))
    short = [short_ref[j] for j in range(3)]
    start = row[:, 0:1]
    first_ref[...] = jnp.broadcast_to(jnp.where(column(row) == start, 1.0, 0.0), (T, T))
    linked = jnp.where(column(before) == start, 1.0, 0.0)

    def rows_of(first):
        return jnp.concatenate([p_ref[first + lane] for lane in range(4)], axis=1)

    own = [h_ref[j - 1] + halo(rows_of((17 + j) * 4), short[j], run8) for j in (1, 2)]
    prev = [rows_of((14 + j) * 4) + halo(rows_of(77 + j * 4), short[j], prev8) for j in (1, 2)]
    e_ref[0:8, :] = jnp.where(linked[0:8] > 0.0, prev[0] * prev[1], 0.0)
    for r in range(15):
        rows = slice(8 * r + 8, 8 * r + 16)
        e_ref[rows, :] = jnp.where(linked[rows] > 0.0, rows_of(r * 4), 0.0)
    e_ref[T : T + 8, :] = own[0] * own[1]
    e_ref[T + 8 : T + 16, :] = jnp.zeros((8, W), F32)
    out_ref[0:8, :] = f0_ref[0:8, :] + halo(rows_of(68), short[0], run8)
    out_ref[8:, :] = f0_ref[8:, :]

    def write(ls, acc):
        for i in range(16):
            rows = slice(8 * i, 8 * i + 8)
            out_ref[rows, ls] = out_ref[rows, ls] * (own_ref[rows, ls] + acc[i])

    def keep(i):
        return first_ref[8 * i : 8 * i + 8, :] > 0.0

    convolve(
        e_ref, s_ref, t_ref, run_ref, (8, T + 16), lambda m: range(0, m), lambda m: range(m, min(16, m + 2)), keep, write
    )


def split(x):
    high = x.astype(jnp.bfloat16)
    return high, (x - high.astype(F32)).astype(jnp.bfloat16)


def dot(a, b, dims):
    return lax.dot_general(a, b, (dims, ((), ())), preferred_element_type=F32)


def attend_kernel(
    place_ref, doc_ref, a0, a1, a2, a3, *rest
):
    kv, late, rest = rest[:12], rest[12:16], rest[16:]
    late = {(3, 0): late[0], (5, 1): late[1], (7, 0): late[2], (7, 1): late[3]}
    outs, (q_ref, kv_ref, sem, k_ref, v_ref, s_ref, qs_ref, p_ref) = rest[:4], rest[4:]
    copies = []

    def fetch(src, dst):
        copies.append(pltpu.make_async_copy(src, dst, sem.at[len(copies)]))
        copies[-1].start()

    early = [(x, t) for x in range(8) for t in range(2) if (x, t) not in late]
    for (x, t), ref in zip(early, kv):
        fetch(ref, kv_ref.at[x, t])
    for i, ref in enumerate((a0, a1, a2, a3)):
        fetch(ref.at[0], q_ref.at[i])
    me = lax.axis_index("seq")
    zq = me // 8
    g = lax.rem(me, 8)

    for x in range(8):
        for t in range(2):
            if (x, t) in early:
                copies[early.index((x, t))].wait()
        for k in range(4):
            at = place_ref[lax.rem(zq + 4 - k, 4) * 8 + lax.bitwise_xor(g, x)]
            rows = pl.ds(pl.multiple_of(at * T, T), T)
            k_ref[rows, :HD], k_ref[rows, HD:] = split(late[x, 0][k] if (x, 0) in late else kv_ref[x, 0, k])
            v_ref[rows, :HD], v_ref[rows, HD:] = split(late[x, 1][k] if (x, 1) in late else kv_ref[x, 1, k])
    for copy in copies[12:]:
        copy.wait()
    scale = 1.0 / jnp.sqrt(jnp.float32(HD))
    causal = iota((T, T), 1) <= iota((T, T), 0)
    home = [place_ref[lax.rem(zq + 4 - i, 4) * 8 + g] for i in range(4)]
    first = [jnp.maximum(c - (NB - 1), 0) for c in home]
    window = [pl.ds(pl.multiple_of(f * T, T), NB * T) for f in first]

    def score(i):
        high, low = split(q_ref[i] * scale)
        qs_ref[i, :T, :HD], qs_ref[i, :T, HD:] = high, high
        qs_ref[i, T:, :HD], qs_ref[i, T:, HD:] = low, jnp.zeros_like(low)
        both = dot(qs_ref[i], k_ref[window[i], :], ((1,), (1,)))
        s_ref[i % 2] = both[:T] + both[T:]

    score(0)
    for i in range(4):
        if i < 3:
            score(i + 1)
        col = column(doc_row(doc_ref, home[i]))
        own = pl.ds(pl.multiple_of((home[i] - first[i]) * T, T), T)
        s_ref[i % 2, :, own] = jnp.where(causal, s_ref[i % 2, :, own], -1e30)
        top = None
        for n in range(NB):
            cols = slice(n * T, n * T + T)
            docs = jnp.where(first[i] + n <= home[i], doc_row(doc_ref, first[i] + n), -1.0)
            s = jnp.where(docs == col, s_ref[i % 2, :, cols], -1e30)
            s_ref[i % 2, :, cols] = s
            top = s if top is None else jnp.maximum(top, s)
        top = jnp.max(top, axis=1, keepdims=True)
        total = jnp.zeros((T, T), F32)
        for n in range(NB):
            cols = slice(n * T, n * T + T)
            p = jnp.exp(s_ref[i % 2, :, cols] - top)
            total = total + p
            p_ref[i % 2, :T, cols], p_ref[i % 2, T:, cols] = split(p)
        acc = dot(p_ref[i % 2], v_ref[window[i], :], ((1,), (0,)))
        acc = acc[:T, :HD] + (acc[:T, HD:] + acc[T:, :HD])
        outs[i][...] = acc / jnp.sum(total, axis=1, keepdims=True)


def join_kernel(hy_ref, a0, a1, a2, a3, out_ref, sq_ref):
    zq = lax.axis_index("seq") // 8
    for k, ref in enumerate((a0, a1, a2, a3)):
        lanes = pl.ds(pl.multiple_of(lax.rem(zq + k, 4) * HD, HD), HD)
        out_ref[:, lanes] = hy_ref[:, lanes] + ref[...]
    y = out_ref[...]
    sq_ref[...] = lax.dot_general(
        jnp.ones((8, W), F32), y * y, (((1,), (1,)), ((), ())), precision=HIGHEST, preferred_element_type=F32
    )


def norm_kernel(y_ref, sq_ref, other_ref, gain_ref, out_ref):
    mean = column(sq_ref[0:1, :] + other_ref[0:1, :]) / (8.0 * W)
    out_ref[...] = y_ref[...] * lax.rsqrt(mean + 1e-05) * gain_ref[...]


def call(kernel, out, ins, scratch=()):
    shapes = [jax.ShapeDtypeStruct(s, F32) for s in out]
    one = len(shapes) == 1
    return pl.pallas_call(
        kernel,
        out_shape=shapes[0] if one else shapes,
        in_specs=ins,
        out_specs=VMEM if one else [VMEM] * len(shapes),
        scratch_shapes=scratch,
    )


def per_device(streams, se_filter, mr_filter, mr_decay, query, key, value, placement_list, doc_ids, norm_gain):
    st = streams.transpose(1, 0, 2)
    se = se_filter.transpose(1, 0, 2)
    mr = mr_filter.T
    docs = doc_ids.reshape(N, T)

    def ring(x, k):
        return lax.ppermute(x, "seq", [(b, (b + 8 * k) % N) for b in range(N)])

    def swap(x, axis, bit):
        return lax.ppermute(x, axis, [(b, b ^ bit) for b in range(N if axis == "seq" else 8)])

    packed = call(pack_kernel, [(3, T, HD)] * 4, [VMEM] * 3)(query, key, value)
    held = [packed[0]] + [None] * 3
    for k in (2, 1, 3):
        held[k] = ring(packed[k], k)

    tiles, f0, gated, heads, short = call(
        local_kernel,
        [(96, 8, 128), (T, W), (T, W), (2, 8, W), (3, SE, W)],
        [SMEM, VMEM, VMEM, VMEM],
        [pltpu.VMEM((3, T + 8, W), F32)],
    )(placement_list, docs, st, se)
    pieces = lax.all_to_all(tiles.reshape(N, 24, 128), "seq", 0, 0, tiled=True)
    conv = [pltpu.VMEM((256, W), F32), pltpu.VMEM((8, 256, W), F32), pltpu.VMEM((T, T), F32)]
    decay = mr_decay.reshape(1, 32)
    own, taps = call(own_kernel, [(T, W), (T, W)], [SMEM] + [VMEM] * 4, conv)(placement_list, docs, mr, decay, gated)

    k0, v0 = (jnp.concatenate([a[t : t + 1] for a in held], axis=0) for t in (1, 2))
    zk = swap(k0, "seq", 4)
    xv = swap(v0, "seq", 2)
    zv = swap(v0, "seq", 4)
    xk = swap(k0, "seq", 2)
    dk = swap(zk, "seq", 2)
    dv = swap(xv, "seq", 4)
    ck, cv = swap(k0, "seq", 1), swap(v0, "seq", 1)
    czk, cxv = swap(zk, "seq", 1), swap(xv, "seq", 1)
    czv, cxk = swap(zv, "seq", 1), swap(xk, "seq", 1)
    cdk, cdv = swap(dk, "seq", 1), swap(dv, "seq", 1)

    chosen = call(select_kernel, [(N, 24, 128)], [SMEM, VMEM], [pltpu.SMEM((N,), jnp.int32)])(
        placement_list, vmem(pieces)
    )
    back = lax.all_to_all(chosen, "seq", 0, 0, tiled=True).reshape(96, 8, 128)

    bf = jnp.bfloat16
    pieces_kv = (k0, v0, ck, cv, xk, xv, cxv, zk, zv, czk, dk, dv)
    near = [hbm(a) for a in (*held[1:], *pieces_kv)]
    near += [vmem(a) for a in (cxk, czv, cdk, cdv)]
    attended = call(
        attend_kernel,
        [(T, HD)] * 4,
        [SMEM, VMEM] + [ANY] * 16 + [VMEM] * 4,
        [
            pltpu.VMEM((4, T, HD), F32),
            pltpu.VMEM((7, 2, 4, T, HD), F32),
            pltpu.SemaphoreType.DMA((16,)),
            *[pltpu.VMEM((N * T, 2 * HD), bf)] * 2,
            pltpu.VMEM((2, T, NB * T), F32),
            pltpu.VMEM((4, 2 * T, 2 * HD), bf),
            pltpu.VMEM((2, 2 * T, NB * T), bf),
        ],
    )(placement_list, docs, held[0], *near)
    home = [attended[0]] + [None] * 3
    for k in (2, 1, 3):
        home[k] = ring(attended[k], -k)

    hyena = call(halo_kernel, [(T, W)], [SMEM] + [VMEM] * 7, [*conv, pltpu.VMEM((T, T), F32)])(
        placement_list, docs, short, taps, f0, own, heads, vmem(back)
    )
    summed, squares = call(join_kernel, [(T, W), (8, 128)], [VMEM] * 5)(hyena, home[0], *map(vmem, home[1:]))

    def along_y(k):
        return lax.ppermute(squares, "mp", [(m, (m + 2 * k) % 8) for m in range(8)])

    squares = squares + along_y(2) + (along_y(1) + along_y(3))
    other = swap(squares, "mp", 1)
    return call(norm_kernel, [(T, W)], [VMEM] * 4)(summed, squares, vmem(other), norm_gain.reshape(1, W))


def solution(mesh):
    placed = (
        P("seq", None, "mp"),
        P(None, None, "mp"),
        P(None, "mp"),
        P("mp"),
        P("seq", "mp"),
        P("seq", "mp"),
        P("seq", "mp"),
        P(),
        P(),
        P("mp"),
    )
    return jax.shard_map(per_device, mesh=mesh, in_specs=placed, out_specs=P("seq", "mp"), check_vma=False)
```
